32 devices in a mesh: pix: 16 (over z, y, core), chan: 2 (over x).
Axes of the slice: x: 2, y: 2, z: 4, core: 2. Of those that a mesh axis runs over, the one named last changes fastest.
Arguments:
- spectra: float32 [32768, 4096], P('pix', 'chan'), may hold values from 0.1 to 3
- coeffs: float32 [32, 32768], P(None, 'pix'), may hold values from 0.05 to 0.5
- endmembers: float32 [32, 4096], P(None, 'chan'), may hold values from 0.05 to 0.5
- pixel_mask: int32 [32768], P('pix'), may hold values from 0 to 1
- labels: int32 [32768], P('pix'), may hold values from 0 to 23
Outputs:
- new_coeffs: float32 [32, 32768], P(None, 'pix')
- new_endmembers: float32 [32, 4096], P(None, 'chan')
- centroids: float32 [24, 4096], P(None, 'chan')
- distances: float32 [32768], P('pix')
The draws below stay inside these ranges and needn't reach their ends.
All inputs are finite; a program needn't handle non-finite values.
Results may differ from the reference program's by a relative error of at most 0.0003.
Values sent between devices are 32-bit elements; how exact they have to be, the bound alone decides.
No kernel may reach another device: no remote copies, remote signals or barrier semaphores. Data moves between devices by JAX's collectives and lax.ppermute only.
A program may use at most 64 MiB of HBM per device.

```python
import math
import jax
import jax.numpy as jnp
from jax import lax

C = 4096
K = 32
PHASES = 24
PIX_DEV = 2048
PIXELS = 32768
N_PIX = 16


def draw_pixel_mask(key, part):
    ranks = jnp.arange(PIXELS, dtype=jnp.int32)
    drawn = jax.random.randint(jax.random.fold_in(key, 17), (PIXELS,), 0, 4 * PIXELS, dtype=jnp.int32)
    return (drawn < PIXELS + 2 * ranks).astype(jnp.int32)


def with_ends(values, key, least, high):
    extent = values.shape
    spot = [jax.random.randint(jax.random.fold_in(key, axis), (), 0, extent[axis]) for axis in range(len(extent))]
    values = values.at[tuple(spot)].set(least)
    longest = extent.index(max(extent))
    spot[longest] = (spot[longest] + 1) % extent[longest]
    return values.at[tuple(spot)].set(high)


def block_scale(stream_key, shape, cuts, smallest, largest):
    level, own = 1.0, jax.random.fold_in(stream_key, 6)
    for axis_at, shards_of in cuts:
        draws = jnp.exp(jax.random.uniform(jax.random.fold_in(own, axis_at), (shards_of,), jnp.float32, smallest / len(cuts), largest / len(cuts)))
        level = level * jnp.repeat(draws, shape[axis_at] // shards_of).reshape([-1 if axis == axis_at else 1 for axis in range(len(shape))])
    return level


def setup_inputs(seed: int = 0) -> dict:
    key_list = jax.random.split(jax.random.key(seed), 6)
    return {
        "spectra": jnp.clip(jnp.exp(math.log(3.0) - 3.4011974 * jax.random.uniform(key_list[0], (PIXELS, C), jnp.float32) ** block_scale(key_list[0], (PIXELS, C), ((0, 16), (1, 2)), -0.2, 0.2)), 0.1, 3.0),
        "coeffs": jnp.clip(jnp.exp(math.log(0.5) - 2.3025851 * jax.random.uniform(key_list[1], (K, PIXELS), jnp.float32) ** block_scale(key_list[1], (K, PIXELS), ((1, 16),), -0.2, 0.2)), 0.05, 0.5),
        "endmembers": jnp.clip(jnp.exp(math.log(0.5) - 2.3025851 * jax.random.uniform(key_list[2], (K, C), jnp.float32) ** block_scale(key_list[2], (K, C), ((1, 2),), -0.2, 0.2)), 0.05, 0.5),
        "pixel_mask": draw_pixel_mask(jax.random.fold_in(key_list[5], 71), 0),
        "labels": with_ends(jax.random.randint(key_list[4], (PIXELS,), 0, PHASES), jax.random.fold_in(key_list[4], 1), 0, PHASES - 1).astype(jnp.int32),
    }


EPSILON = 1e-6


def product(left, right):
    return jnp.dot(left, right, precision=lax.Precision.HIGHEST, preferred_element_type=jnp.float32)


def reference(spectra, coeffs, endmembers, pixel_mask, labels):
    numer_coeff = product(endmembers, spectra.T)
    gram_all = product(endmembers, endmembers.T)
    new_coeffs = coeffs * numer_coeff / (product(gram_all, coeffs) + EPSILON)
    weights = pixel_mask.astype(jnp.float32)
    weighted = new_coeffs * weights[None, :]
    numer_end = product(weighted, spectra)
    outer_gram = product(weighted, new_coeffs.T)
    new_endmembers = endmembers * numer_end / (product(outer_gram, endmembers) + EPSILON)
    onehot = (labels[None, :] == jnp.arange(PHASES, dtype=jnp.int32)[:, None]).astype(jnp.float32)
    picked = onehot * weights[None, :]
    phase_sums = product(picked, new_coeffs.T)
    phase_counts = jnp.sum(picked, axis=1)
    phase_means = phase_sums / (phase_counts + 1.0)[:, None]
    centroids = product(phase_means, new_endmembers)
    coeff_blocks = new_coeffs.reshape(K, N_PIX, PIX_DEV).transpose(1, 0, 2)
    label_blocks = onehot.reshape(PHASES, N_PIX, PIX_DEV).transpose(1, 0, 2)

    def block_distance(pieces):
        block_coeffs, block_onehot = pieces
        rebuilt = product(block_coeffs.T, new_endmembers)
        target = product(block_onehot.T, centroids)
        return jnp.sum((rebuilt - target) ** 2, axis=1) / C

    distances = lax.map(block_distance, (coeff_blocks, label_blocks)).reshape(PIXELS)
    return new_coeffs, new_endmembers, centroids, distances
```

```python
import jax
import jax.numpy as jnp
from jax import lax
from jax.experimental import pallas as pl
from jax.experimental.pallas import tpu as pltpu
from jax.sharding import PartitionSpec as P

PHASES = 24
EPSILON = 1e-06
TILE = 128
LOOKAHEAD = 3


F32 = jnp.float32
BF16 = jnp.bfloat16
VMEM = pl.BlockSpec(memory_space=pltpu.VMEM)
HBM = pl.BlockSpec(memory_space=pl.ANY)


def dot(left, right, left_dim, right_dim):
    return lax.dot_general(
        left,
        right,
        (((left_dim,), (right_dim,)), ((), ())),
        precision=lax.Precision.HIGHEST,
        preferred_element_type=F32,
    )


def dot_bf16(left, right, left_dim, right_dim):
    return lax.dot_general(
        left, right, (((left_dim,), (right_dim,)), ((), ())), preferred_element_type=F32
    )


def split(value):
    high = value.astype(BF16)
    low = (value - high.astype(F32)).astype(BF16)
    return high, low


def stacked(value):
    return jnp.concatenate(split(value), axis=0)


def streamed(spectra, buffer, sems, first, step, count):
    copies = [
        pltpu.make_async_copy(
            spectra.at[pl.ds(first + i * step, step)],
            buffer.at[pl.ds(i * step, step)],
            sems.at[i],
        )
        for i in range(count)
    ]
    for i in range(min(LOOKAHEAD, count)):
        copies[i].start()

    def block(i):
        copies[i].wait()
        if i + LOOKAHEAD < count:
            copies[i + LOOKAHEAD].start()
        return split(buffer[i * step : (i + 1) * step, :])

    return block


def rows_per_block(rows):
    return 256 if rows % 256 == 0 else rows


def numerator(spectra, endmembers, first, rows):
    members, channels = endmembers.shape
    step = rows_per_block(rows)
    count = rows // step

    def kernel(ends_ref, spectra_ref, out_ref, buffer, sems):
        block = streamed(spectra_ref, buffer, sems, first, step, count)
        ends = stacked(ends_ref[...])
        gram = dot_bf16(ends, ends, 1, 1)
        gram = gram[:members] + gram[members:]
        gram = gram[:, :members] + gram[:, members:]
        out_ref[:, rows:] = jnp.concatenate(
            [gram, jnp.zeros((members, TILE - members), F32)], axis=1
        )
        for i in range(count):
            high, low = block(i)
            part = dot_bf16(high, ends, 1, 1) + dot_bf16(low, ends, 1, 1)
            part = part.T
            out_ref[:, i * step : (i + 1) * step] = part[:members] + part[members:]

    return pl.pallas_call(
        kernel,
        in_specs=[VMEM, HBM],
        out_specs=VMEM,
        out_shape=jax.ShapeDtypeStruct((members, rows + TILE), F32),
        scratch_shapes=[
            pltpu.VMEM((rows, channels), F32),
            pltpu.SemaphoreType.DMA((count,)),
        ],
        compiler_params=pltpu.CompilerParams(vmem_limit_bytes=40 << 20),
        name="numerator",
    )(endmembers, spectra)


def update(spectra, sums, gram, coeffs, mask, labels, first, rows):
    members = coeffs.shape[0]
    channels = spectra.shape[1]
    step = rows_per_block(rows)
    count = rows // step

    def kernel(spectra_ref, sums_ref, gram_ref, coeffs_ref, mask_ref, labels_ref, new_ref, end_ref, tile_ref, buffer, sems):
        block = streamed(spectra_ref, buffer, sems, first, step, count)
        old = coeffs_ref[...]
        new = old * sums_ref[...] / (dot(gram_ref[...], old, 1, 0) + EPSILON)
        new_ref[...] = new
        weight = mask_ref[...].astype(F32)
        weighted = new * weight
        terms = stacked(weighted)
        phase = lax.broadcasted_iota(jnp.int32, (members, rows), 0)
        picked = jnp.where(phase == labels_ref[...], weight, 0.0)
        counts = jnp.sum(picked, axis=1, keepdims=True)
        both = dot(jnp.concatenate([weighted, picked], axis=0), new, 1, 1)
        tile_ref[...] = jnp.concatenate(
            [both[:members], both[members:], jnp.broadcast_to(counts, (members, TILE - 2 * members))], axis=1
        )
        total = None
        for i in range(count):
            high, low = block(i)
            left = terms[:, i * step : (i + 1) * step]
            part = dot_bf16(left, high, 1, 0) + dot_bf16(left, low, 1, 0)
            total = part if total is None else total + part
        end_ref[...] = total[:members] + total[members:]

    return pl.pallas_call(
        kernel,
        in_specs=[HBM] + [VMEM] * 5,
        out_specs=[VMEM] * 3,
        out_shape=[
            jax.ShapeDtypeStruct((members, rows), F32),
            jax.ShapeDtypeStruct((members, channels), F32),
            jax.ShapeDtypeStruct((members, TILE), F32),
        ],
        scratch_shapes=[
            pltpu.VMEM((rows, channels), F32),
            pltpu.SemaphoreType.DMA((count,)),
        ],
        compiler_params=pltpu.CompilerParams(vmem_limit_bytes=40 << 20),
        name="update",
    )(spectra, sums, gram, coeffs, mask, labels)


def partner(value, axis, bit):
    pairs = [(i, i ^ bit) for i in range(lax.axis_size(axis))]
    return lax.ppermute(value, axis, pairs)


def bits(axis, first=1):
    size = lax.axis_size(axis)
    if size & (size - 1):
        raise ValueError("axis size")
    found = []
    while first < size:
        found.append(first)
        first *= 2
    return found


def summed(value, axis, first=1):
    for bit in bits(axis, first):
        value = value + partner(value, axis, bit)
    return value


def local(spectra, coeffs, endmembers, pixel_mask, labels):
    pixels, channels = spectra.shape
    members = coeffs.shape[0]
    channels_total = channels * lax.axis_size("chan")
    half = channels // 2
    core = lax.rem(lax.axis_index("pix"), 2)

    mask_row = pixel_mask[None, :]
    label_row = labels[None, :]
    sums = summed(numerator(spectra, endmembers, 0, pixels), "chan")
    gram = sums[:, pixels : pixels + members]
    new_coeffs, numer_end, tile = update(
        spectra, sums[:, :pixels], gram, coeffs, mask_row, label_row, 0, pixels
    )

    mine = jnp.where(core == 0, numer_end[:, :half], numer_end[:, half:])
    other = jnp.where(core == 0, numer_end[:, half:], numer_end[:, :half])
    total = jnp.concatenate([mine, tile], axis=1) + partner(
        jnp.concatenate([other, tile], axis=1), "pix", 1
    )
    total = summed(total, "pix", 2)
    outer_gram = total[:, half : half + members]
    phase_sums = total[:PHASES, half + members : half + 2 * members]
    phase_counts = total[:PHASES, half + 2 * members : half + 2 * members + 1]

    ends_mine = jnp.where(core == 0, endmembers[:, :half], endmembers[:, half:])
    new_mine = ends_mine * total[:, :half] / (dot(outer_gram, ends_mine, 1, 0) + EPSILON)
    new_other = partner(new_mine, "pix", 1)
    gram_mine = summed(dot(new_mine, new_mine, 1, 1), "chan")
    gram_new = gram_mine + partner(gram_mine, "pix", 1)
    new_endmembers = jnp.concatenate(
        [jnp.where(core == 0, new_mine, new_other), jnp.where(core == 0, new_other, new_mine)], axis=1
    )
    phase_means = phase_sums / (phase_counts + 1.0)
    centroids = dot(phase_means, new_endmembers, 1, 0)
    onehot = (labels[None, :] == jnp.arange(PHASES, dtype=jnp.int32)[:, None]).astype(F32)
    offset = new_coeffs - dot(phase_means, onehot, 0, 0)
    distance = jnp.sum(offset * dot(gram_new, offset, 1, 0), axis=0) / channels_total
    return (new_coeffs, new_endmembers, centroids, distance)


def solution(mesh):
    placed = (P("pix", "chan"), P(None, "pix"), P(None, "chan"), P("pix"), P("pix"))
    return jax.shard_map(
        local,
        mesh=mesh,
        in_specs=placed,
        out_specs=(P(None, "pix"), P(None, "chan"), P(None, "chan"), P("pix")),
        check_vma=False,
    )
```

```python
import jax
import jax.numpy as jnp
from jax import lax
from jax.experimental import pallas as pl
from jax.experimental.pallas import tpu as pltpu
from jax.sharding import PartitionSpec as P


PHASES = 24
EPSILON = 1e-06
TILE = 128
AHEAD = 4
CORE, NEAR, FAR = 1, 2, 4


F32 = jnp.float32
BF16 = jnp.bfloat16
VMEM = pl.BlockSpec(memory_space=pltpu.VMEM)
HBM = pl.BlockSpec(memory_space=pl.ANY)


def dot(left, right, left_dim, right_dim):
    return lax.dot_general(
        left,
        right,
        (((left_dim,), (right_dim,)), ((), ())),
        precision=lax.Precision.HIGHEST,
        preferred_element_type=F32,
    )


def dot_bf16(left, right, left_dim, right_dim):
    return lax.dot_general(
        left, right, (((left_dim,), (right_dim,)), ((), ())), preferred_element_type=F32
    )


def split(value):
    high = value.astype(BF16)
    low = (value - high.astype(F32)).astype(BF16)
    return high, low


def stacked(value):
    return jnp.concatenate(split(value), axis=0)


def in_vmem(value):
    return pltpu.with_memory_space_constraint(value, pltpu.VMEM)


def in_hbm(value):
    return pltpu.with_memory_space_constraint(value, pltpu.HBM)


def columns_per_block(channels):
    return 256 if channels % 256 == 0 else channels


def numerator(spectra, endmembers, first, rows, with_gram):
    channels = spectra.shape[1]
    members = endmembers.shape[0]
    step = columns_per_block(channels)
    count = channels // step
    extra = TILE if with_gram else 0

    def kernel(ends_hbm, spectra_hbm, out_ref, high_ref, low_ref, ends_ref, buffer, sems):
        copies = [
            pltpu.make_async_copy(
                spectra_hbm.at[pl.ds(first, rows), pl.ds(i * step, step)], buffer.at[i % AHEAD], sems.at[i]
            )
            for i in range(count)
        ]
        ends_copy = pltpu.make_async_copy(ends_hbm, ends_ref, sems.at[count])
        ends_copy.start()
        for i in range(min(AHEAD, count)):
            copies[i].start()
        ends_copy.wait()
        ends = stacked(ends_ref[...])
        if with_gram:
            gram = dot_bf16(ends, ends, 1, 1)
            gram = gram[:members] + gram[members:]
            gram = gram[:, :members] + gram[:, members:]
            out_ref[:, rows:] = jnp.concatenate(
                [gram, jnp.zeros((members, TILE - members), F32)], axis=1
            )
        total = None
        for i in range(count):
            copies[i].wait()
            high, low = split(buffer[i % AHEAD])
            if i + AHEAD < count:
                copies[i + AHEAD].start()
            high_ref[:, i * step : (i + 1) * step] = high
            low_ref[:, i * step : (i + 1) * step] = low
            left = ends[:, i * step : (i + 1) * step]
            part = dot_bf16(left, high, 1, 1) + dot_bf16(left, low, 1, 1)
            total = part if total is None else total + part
        out_ref[:, :rows] = total[:members] + total[members:]

    return pl.pallas_call(
        kernel,
        in_specs=[HBM, HBM],
        out_specs=[VMEM] * 3,
        out_shape=[
            jax.ShapeDtypeStruct((members, rows + extra), F32),
            pltpu.VMEM((rows, channels), BF16),
            pltpu.VMEM((rows, channels), BF16),
        ],
        scratch_shapes=[
            pltpu.VMEM((members, channels), F32),
            pltpu.VMEM((AHEAD, rows, step), F32),
            pltpu.SemaphoreType.DMA((count + 1,)),
        ],
        compiler_params=pltpu.CompilerParams(vmem_limit_bytes=20 << 20),
        cost_estimate=pl.CostEstimate(
            flops=8 * members * rows * channels, bytes_accessed=8 * rows * channels, transcendentals=0
        ),
        name="numerator",
    )(in_hbm(endmembers), in_hbm(spectra))


def update(high, low, sums, gram, coeffs, mask, labels, before=()):
    members, pixels = coeffs.shape
    channels = high.shape[1]

    def kernel(high_ref, low_ref, sums_ref, gram_ref, coeffs_ref, mask_ref, labels_ref, *refs):
        new_ref, tile_ref, end_ref = refs[-3:]
        old = coeffs_ref[...]
        new = old * sums_ref[...] / (dot(gram_ref[...], old, 1, 0) + EPSILON)
        new_ref[...] = new
        weight = mask_ref[...].astype(F32)
        weighted = new * weight
        terms = stacked(weighted)
        phase = lax.broadcasted_iota(jnp.int32, (members, pixels), 0)
        picked = jnp.where(phase == labels_ref[...], weight, 0.0)
        counts = jnp.sum(picked, axis=1, keepdims=True)
        both = dot(jnp.concatenate([weighted, picked], axis=0), new, 1, 1)
        tile = jnp.concatenate(
            [both[:members], both[members:], jnp.broadcast_to(counts, (members, TILE - 2 * members))], axis=1
        )
        left = jnp.concatenate([terms, terms], axis=1)
        right = jnp.concatenate([high_ref[...], low_ref[...]], axis=0)
        part = dot_bf16(left, right, 1, 0)
        end = part[:members] + part[members:]
        if before:
            tile = tile + refs[0][...]
            end = end + refs[1][...]
        tile_ref[...] = tile
        end_ref[...] = end

    return pl.pallas_call(
        kernel,
        in_specs=[VMEM] * (7 + len(before)),
        out_specs=[VMEM] * 3,
        out_shape=[
            jax.ShapeDtypeStruct((members, pixels), F32),
            jax.ShapeDtypeStruct((members, TILE), F32),
            jax.ShapeDtypeStruct((members, channels), F32),
        ],
        compiler_params=pltpu.CompilerParams(vmem_limit_bytes=16 << 20),
        cost_estimate=pl.CostEstimate(
            flops=8 * members * pixels * channels, bytes_accessed=4 * pixels * channels, transcendentals=0
        ),
        name="update",
    )(in_vmem(high), in_vmem(low), sums, gram, coeffs, mask, labels, *before)


def partner(value, axis, bit):
    pairs = [(i, i ^ bit) for i in range(lax.axis_size(axis))]
    return lax.ppermute(value, axis, pairs)


def bits(axis, first=1):
    size = lax.axis_size(axis)
    if size & (size - 1):
        raise ValueError("axis size")
    found = []
    while first < size:
        found.append(first)
        first *= 2
    return found


def summed(value, axis, order):
    for bit in order:
        value = value + partner(value, axis, bit)
    return value


def across(value, bit):
    pix, chan = lax.axis_size("pix"), lax.axis_size("chan")
    pairs = [
        (i * chan + j, (i ^ bit) * chan + (j ^ 1)) for i in range(pix) for j in range(chan)
    ]
    return lax.ppermute(value, ("pix", "chan"), pairs)


def halved(value, low):
    width = value.shape[1] // 2
    left, right = value[:, :width], value[:, width:]
    return jnp.where(low, left, right), jnp.where(low, right, left)


def joined(mine, other, low):
    return jnp.concatenate([jnp.where(low, mine, other), jnp.where(low, other, mine)], axis=1)


def beside(*values):
    return jnp.concatenate(values, axis=1)


def local(spectra, coeffs, endmembers, pixel_mask, labels):
    pixels, channels = spectra.shape
    members = coeffs.shape[0]
    channels_total = channels * lax.axis_size("chan")
    chan_bits = bits("chan")
    half = pixels // 2
    mask_row, label_row = pixel_mask[None, :], labels[None, :]

    index = lax.axis_index("pix")
    core_low = jnp.bitwise_and(index, CORE) == 0
    near_low = jnp.bitwise_and(index, NEAR) == 0
    endmembers, core_low, near_low = lax.optimization_barrier((endmembers, core_low, near_low))

    sums_a, high_a, low_a = numerator(spectra, endmembers, 0, half, True)
    sums_b, high_b, low_b = numerator(spectra, endmembers, half, half, False)
    sums_a = summed(sums_a, "chan", chan_bits)
    sums_b = summed(sums_b, "chan", chan_bits)
    gram = sums_a[:, half : half + members]
    new_a, tile_a, end_a = update(
        high_a, low_a, sums_a[:, :half], gram, coeffs[:, :half], mask_row[:, :half], label_row[:, :half]
    )
    new_b, tile, end = update(
        high_b, low_b, sums_b, gram, coeffs[:, half:], mask_row[:, half:], label_row[:, half:], (tile_a, end_a)
    )
    new_coeffs = beside(new_a, new_b)

    mine, other = halved(end, core_low)
    total = beside(mine, tile) + partner(beside(other, tile), "pix", CORE)
    width = mine.shape[1]
    mine, other = halved(total[:, :width], near_low)
    tile = total[:, width:]
    total = beside(mine, tile) + partner(beside(other, tile), "pix", NEAR)
    total = summed(total, "pix", bits("pix", FAR))
    width = mine.shape[1]
    outer_gram = total[:, width : width + members]
    phase_sums = total[:PHASES, width + members : width + 2 * members]
    phase_counts = total[:PHASES, width + 2 * members : width + 2 * members + 1]

    ends = halved(halved(endmembers, core_low)[0], near_low)[0]
    new = ends * total[:, :width] / (dot(outer_gram, ends, 1, 0) + EPSILON)
    gram_new = dot(new, new, 1, 1)
    padding = jnp.zeros((members, TILE - members), F32)
    got = partner(beside(new, gram_new, padding), "pix", NEAR)
    from_chan = partner(gram_new, "chan", 1)
    from_both = across(gram_new, NEAR)
    gram_new = gram_new + from_chan + from_both + got[:, width : width + members]
    new = joined(new, got[:, :width], near_low)
    gram_new = summed(gram_new, "chan", chan_bits[1:])
    new_endmembers = joined(new, partner(new, "pix", CORE), core_low)
    gram_new = gram_new + partner(gram_new, "pix", CORE)
    phase_means = phase_sums / (phase_counts + 1.0)
    centroids = dot(phase_means, new_endmembers, 1, 0)
    onehot = (labels[None, :] == jnp.arange(PHASES, dtype=jnp.int32)[:, None]).astype(F32)
    offset = new_coeffs - dot(phase_means, onehot, 0, 0)
    distance = jnp.sum(offset * dot(gram_new / channels_total, offset, 1, 0), axis=0)
    return (new_coeffs, new_endmembers, centroids, distance)


def solution(mesh):
    placed = (P("pix", "chan"), P(None, "pix"), P(None, "chan"), P("pix"), P("pix"))
    return jax.shard_map(
        local,
        mesh=mesh,
        in_specs=placed,
        out_specs=(P(None, "pix"), P(None, "chan"), P(None, "chan"), P("pix")),
        check_vma=False,
    )
```
